32 devices in a mesh: dp: 2 (over x), hst: 4 (over y, core), chip: 4 (over z).
Axes of the slice: x: 2, y: 2, z: 4, core: 2. Of those that a mesh axis runs over, the one named last changes fastest.
Arguments:
- tokens: bfloat16 [512, 8192], P('dp', ('hst', 'chip')), may hold values from -6 to 6
- out_grad: bfloat16 [512, 8192], P('dp', ('hst', 'chip')), may hold values from -6 to 6
- up_blocks: bfloat16 [112, 16, 128, 128], P(('hst', 'chip')), may hold values from -0.125 to 0.125
- up_cols: int32 [112, 16], P(('hst', 'chip')), may hold values from 0 to 63, all different within a row
- down_blocks: bfloat16 [112, 16, 128, 128], P(('hst', 'chip')), may hold values from -0.09375 to 0.09375
- down_cols: int32 [112, 16], P(('hst', 'chip')), may hold values from 0 to 63, all different within a row
Outputs:
- input_grad: bfloat16 [512, 8192], P('dp', ('hst', 'chip'))
- up_grad: float32 [112, 16, 128, 128], P(('hst', 'chip'), None, 'dp')
- down_grad: float32 [112, 16, 128, 128], P(('hst', 'chip'), None, 'dp')
The draws below stay inside these ranges and needn't reach their ends.
Inputs may be any that keep to these rules, and one draw needn't show every extreme that they name: `up_cols`: each block row names 16 different block columns; every block column is named by some row. `down_cols`: each block row names 16 different block columns; every block column is named by some row.
All inputs are finite; a program needn't handle non-finite values.
Results may differ from the reference program's by a relative error of at most 0.017.
Values may be sent and summed in bfloat16 or wider, within the bound.
A program may use at most 128 MiB of HBM per device.

```python
import jax
import jax.numpy as jnp
from jax import lax

D = 8192
FF = 14336
BLK = 128
K = 16
TOK_DEV = 256
TOKENS = 512
HB = 112
N_DP = 2
N_HST = 4
N_CHIP = 4


def level_of(rng, shape, cuts, smallest, largest):
    level, own = 1.0, jax.random.fold_in(rng, 6)
    for position, parts in cuts:
        heights = jnp.exp(jax.random.uniform(jax.random.fold_in(own, position), (parts,), jnp.float32, smallest / len(cuts), largest / len(cuts)))
        level = level * jnp.repeat(heights, shape[position] // parts).reshape([-1 if axis == position else 1 for axis in range(len(shape))])
    return level


def different_ones(own_key, rows, amount, top, lift):
    ranking = jax.random.permutation(jax.random.fold_in(own_key, 1), amount)
    boost = ranking
    for power in range(3):
        boost = boost * boost // amount
    boost = boost * lift // amount
    chance = jax.random.randint(jax.random.fold_in(own_key, 2), (rows, amount), 0, 4096) + boost
    fixed_rows = jax.random.permutation(jax.random.fold_in(own_key, 3), rows)[jnp.arange(amount) % rows]
    chance = jnp.where(jnp.arange(rows)[:, None] == fixed_rows[None, :], 1 << 14, chance)
    score = chance * amount + jnp.arange(amount)
    return lax.top_k(score.astype(jnp.int32), top)[1].astype(jnp.int32)


def bell_draw(own_key, shape, deviation, bound, pieces=(), kind=jnp.bfloat16):
    values = jax.random.normal(own_key, shape, jnp.float32) * deviation
    if len(pieces) > 0:
        values = level_of(own_key, shape, pieces, -0.22, 0.18) * values
    return jnp.clip(values, min=-bound, max=bound).astype(kind)


def setup_inputs(seed: int = 0) -> dict:
    seeds = jax.random.split(jax.random.key(seed), 7)
    return {
        "tokens": bell_draw(seeds[0], (TOKENS, D), 1.0, 6.0, ((0, 2), (1, 16))),
        "out_grad": bell_draw(seeds[1], (TOKENS, D), 1.0, 6.0, ((0, 2), (1, 16))),
        "up_blocks": bell_draw(seeds[2], (HB, K, BLK, BLK), (K * BLK) ** -0.5, 0.125, ((0, 16),)),
        "up_cols": different_ones(seeds[3], HB, D // BLK, K, 4096),
        "down_blocks": bell_draw(seeds[4], (HB, K, BLK, BLK), (FF // 4) ** -0.5, 0.09375, ((0, 16),)),
        "down_cols": different_ones(seeds[5], HB, D // BLK, K, 4096),
    }


def reference(tokens, out_grad, up_blocks, up_cols, down_blocks, down_cols):
    dblocks = D // BLK
    shards = N_HST * N_CHIP
    rows_each = HB // shards
    x_blocks = tokens.reshape(N_DP, TOK_DEV, dblocks, BLK)
    dy_blocks = out_grad.reshape(N_DP, TOK_DEV, dblocks, BLK)
    columns = jnp.arange(dblocks, dtype=jnp.int32)

    def row_step(carried, per_row):
        up_row, up_idx, down_row, down_idx = per_row
        x_sel = x_blocks[:, :, up_idx, :].astype(jnp.float32)
        dy_sel = dy_blocks[:, :, down_idx, :].astype(jnp.float32)
        up_f = up_row.astype(jnp.float32)
        down_f = down_row.astype(jnp.float32)
        pre_act = jnp.einsum('gtkc,khc->gth', x_sel, up_f)
        activated = jax.nn.silu(pre_act).astype(jnp.bfloat16)
        down_part = jnp.einsum('gth,gtkc->gkhc', activated.astype(jnp.float32), dy_sel).astype(jnp.bfloat16)
        down_part = lax.optimization_barrier(down_part)
        down_sum = jnp.sum(down_part.astype(jnp.float32), axis=0)
        hidden_grad = jnp.einsum('gtkc,khc->gth', dy_sel, down_f)
        sigmoid_pre = jax.nn.sigmoid(pre_act)
        pre_grad = (hidden_grad * sigmoid_pre * (1.0 + pre_act * (1.0 - sigmoid_pre))).astype(jnp.bfloat16)
        pre_float = pre_grad.astype(jnp.float32)
        up_part = jnp.einsum('gth,gtkc->gkhc', pre_float, x_sel).astype(jnp.bfloat16)
        up_part = lax.optimization_barrier(up_part)
        up_sum = jnp.sum(up_part.astype(jnp.float32), axis=0)
        contrib = jnp.einsum('gth,khc->gtkc', pre_float, up_f).reshape(TOKENS, K, BLK)
        onehot = (up_idx[:, None] == columns[None, :]).astype(jnp.float32)
        carried = carried + jnp.einsum('tkc,kb->tbc', contrib, onehot, precision=lax.Precision.HIGHEST)
        return carried, (up_sum, down_sum)

    def shard_step(total, per_shard):
        start = jnp.zeros((TOKENS, dblocks, BLK), jnp.float32)
        partial_value, grads = lax.scan(row_step, start, per_shard)
        rounded = lax.optimization_barrier(partial_value.astype(jnp.bfloat16))
        return total + rounded.astype(jnp.float32), grads

    grouped = (up_blocks.reshape(shards, rows_each, K, BLK, BLK),
               up_cols.astype(jnp.int32).reshape(shards, rows_each, K),
               down_blocks.reshape(shards, rows_each, K, BLK, BLK),
               down_cols.astype(jnp.int32).reshape(shards, rows_each, K))
    begin = jnp.zeros((TOKENS, dblocks, BLK), jnp.float32)
    total, grads = lax.scan(shard_step, begin, grouped)
    input_grad = total.reshape(TOKENS, D).astype(jnp.bfloat16)
    up_grad = grads[0].reshape(HB, K, BLK, BLK)
    down_grad = grads[1].reshape(HB, K, BLK, BLK)
    return input_grad, up_grad, down_grad
```

```python
import functools

import jax
import jax.numpy as jnp
from jax import lax
from jax.experimental import pallas as pl
from jax.experimental.pallas import tpu as pltpu
from jax.sharding import PartitionSpec as P

NT = (((1,), (1,)), ((), ()))


def rows_kernel(
    split,
    up_cols,
    down_cols,
    me,
    x_ref,
    dy_ref,
    up_ref,
    down_ref,
    in_ref,
    *rest,
):
    outs, (acc, xs, dys, us, ds) = rest[:-5], rest[-5:]
    row = pl.program_id(0)
    width = up_ref.shape[-1]
    per_shard = x_ref.shape[2] // width
    count = up_ref.shape[1]

    @pl.when(row == 0)
    def _():
        acc[...] = jnp.zeros_like(acc)

    def place(col):
        return col // per_shard, pl.ds(pl.multiple_of((col % per_shard) * width, width), width)

    for k in range(count):
        lanes = pl.ds(k * width, width)
        shard, at = place(up_cols[row, k])
        xs[:, lanes] = x_ref[shard, :, at]
        shard, at = place(down_cols[row, k])
        dys[:, lanes] = dy_ref[shard, :, at]
        us[:, lanes] = up_ref[0, k]
        ds[:, lanes] = down_ref[0, k]
    pre = lax.dot_general(us[...], xs[...], NT, preferred_element_type=jnp.float32)
    hid = lax.dot_general(ds[...], dys[...], NT, preferred_element_type=jnp.float32)
    sig = 1.0 / (1.0 + jnp.exp(-pre))
    act = (pre * sig).astype(jnp.bfloat16)
    pre_grad_f = hid * sig * (1.0 + pre * (1.0 - sig))
    pre_grad = pre_grad_f.astype(jnp.bfloat16)
    pre_grad_t = pre_grad_f.T.astype(jnp.bfloat16)

    step = 4
    for base in range(0, count, step):
        lanes = pl.ds(base * width, step * width)
        up_part = jnp.dot(pre_grad, xs[:, lanes], preferred_element_type=jnp.float32)
        down_part = jnp.dot(act, dys[:, lanes], preferred_element_type=jnp.float32)
        back = jnp.dot(pre_grad_t, us[:, lanes], preferred_element_type=jnp.float32)
        for i in range(step):
            k = base + i
            cut = slice(i * width, (i + 1) * width)
            for part, out in ((up_part, outs[: len(outs) // 2]), (down_part, outs[len(outs) // 2 :])):
                block = part[:, cut].astype(jnp.bfloat16)
                if split:
                    half = width // 2
                    first = me[0] == 0
                    out[0][0, k] = jnp.where(first, block[:half], block[half:])
                    out[1][0, k] = jnp.where(first, block[half:], block[:half])
                else:
                    out[0][0, k] = block
            shard, at = place(up_cols[row, k])
            acc[shard, :, at] += back[:, cut]

    @pl.when(row == pl.num_programs(0) - 1)
    def _():
        for s in range(acc.shape[0]):
            in_ref[s] = acc[s].astype(jnp.bfloat16)


def rows_call(split, whole_x, whole_dy, up_blocks, up_cols, down_blocks, down_cols):
    rows, count, width, _ = up_blocks.shape
    shards, tok, part = whole_x.shape
    out_h = width // 2 if split else width
    n_out = 4 if split else 2
    whole = pl.BlockSpec(memory_space=pltpu.VMEM)
    smem = pl.BlockSpec(memory_space=pltpu.SMEM)

    def block(h):
        return pl.BlockSpec((1, count, h, width), lambda r: (r, 0, 0, 0))

    me = lax.axis_index("dp").astype(jnp.int32).reshape(1)
    flops = 10 * tok * rows * count * width * width
    return pl.pallas_call(
        functools.partial(rows_kernel, split),
        grid=(rows,),
        in_specs=[smem, smem, smem, whole, whole, block(width), block(width)],
        out_specs=[whole] + [block(out_h)] * n_out,
        out_shape=[jax.ShapeDtypeStruct(whole_x.shape, jnp.bfloat16)]
        + [jax.ShapeDtypeStruct((rows, count, out_h, width), jnp.bfloat16)] * n_out,
        scratch_shapes=[
            pltpu.VMEM(whole_x.shape, jnp.float32),
            pltpu.VMEM((tok, count * width), jnp.bfloat16),
            pltpu.VMEM((tok, count * width), jnp.bfloat16),
            pltpu.VMEM((width, count * width), jnp.bfloat16),
            pltpu.VMEM((width, count * width), jnp.bfloat16),
        ],
        compiler_params=pltpu.CompilerParams(
            dimension_semantics=("arbitrary",), vmem_limit_bytes=56 * 2**20
        ),
        cost_estimate=pl.CostEstimate(
            flops=flops, bytes_accessed=30 * 2**20, transcendentals=rows * width * tok
        ),
    )(up_cols, down_cols, me, whole_x, whole_dy, up_blocks, down_blocks)


def local(n_dp, tokens, out_grad, up_blocks, up_cols, down_blocks, down_cols):
    whole_x = lax.all_gather(tokens, ("hst", "chip"), axis=0, tiled=False)
    whole_dy = lax.all_gather(out_grad, ("hst", "chip"), axis=0, tiled=False)
    split = n_dp == 2
    partial_value, *grads = rows_call(
        split, whole_x, whole_dy, up_blocks, up_cols, down_blocks, down_cols
    )
    if split:
        swap = [(0, 1), (1, 0)]
        sums = [
            grads[i].astype(jnp.float32)
            + lax.ppermute(grads[i + 1], "dp", swap).astype(jnp.float32)
            for i in (0, 2)
        ]
    else:
        sums = [
            lax.psum_scatter(g, "dp", scatter_dimension=2, tiled=True).astype(jnp.float32)
            for g in grads
        ]
    summed = lax.psum_scatter(
        partial_value, ("hst", "chip"), scatter_dimension=0, tiled=False
    )
    return (summed, *sums)


def solution(mesh):
    placed = (
        P("dp", ("hst", "chip")),
        P("dp", ("hst", "chip")),
        P(("hst", "chip"), None, None, None),
        P(("hst", "chip"), None),
        P(("hst", "chip"), None, None, None),
        P(("hst", "chip"), None),
    )
    return jax.shard_map(
        functools.partial(local, mesh.shape["dp"]),
        mesh=mesh,
        in_specs=placed,
        out_specs=(
            P("dp", ("hst", "chip")),
            P(("hst", "chip"), None, "dp", None),
            P(("hst", "chip"), None, "dp", None),
        ),
        check_vma=False,
    )
```

```python
import functools

import jax
import jax.numpy as jnp
from jax import lax
from jax.experimental import pallas as pl
from jax.experimental.pallas import tpu as pltpu
from jax.sharding import PartitionSpec as P

NT = (((1,), (1,)), ((), ()))


def rows_kernel(
    split,
    up_cols,
    down_cols,
    me,
    x_ref,
    dy_ref,
    up_ref,
    down_ref,
    in_ref,
    *rest,
):
    outs, (acc, xs, dys, us, ds) = rest[:-5], rest[-5:]
    row = pl.program_id(0)
    width = up_ref.shape[-1]
    per_shard = x_ref.shape[2] // width
    count = up_ref.shape[1]

    @pl.when(row == 0)
    def _():
        acc[...] = jnp.zeros_like(acc)

    def place(col):
        return col // per_shard, pl.ds(pl.multiple_of((col % per_shard) * width, width), width)

    for k in range(count):
        lanes = pl.ds(k * width, width)
        shard, at = place(up_cols[row, k])
        xs[:, lanes] = x_ref[shard, :, at]
        shard, at = place(down_cols[row, k])
        dys[:, lanes] = dy_ref[shard, :, at]
        us[:, lanes] = up_ref[0, k]
        ds[:, lanes] = down_ref[0, k]
    pre = lax.dot_general(us[...], xs[...], NT, preferred_element_type=jnp.float32)
    hid = lax.dot_general(ds[...], dys[...], NT, preferred_element_type=jnp.float32)
    sig = 1.0 / (1.0 + jnp.exp(-pre))
    act = (pre * sig).astype(jnp.bfloat16)
    pre_grad_f = hid * sig * (1.0 + pre * (1.0 - sig))
    pre_grad = pre_grad_f.astype(jnp.bfloat16)
    pre_grad_t = pre_grad_f.T.astype(jnp.bfloat16)

    step = 4
    for base in range(0, count, step):
        lanes = pl.ds(base * width, step * width)
        up_part = jnp.dot(pre_grad, xs[:, lanes], preferred_element_type=jnp.float32)
        down_part = jnp.dot(act, dys[:, lanes], preferred_element_type=jnp.float32)
        back = jnp.dot(pre_grad_t, us[:, lanes], preferred_element_type=jnp.float32)
        for i in range(step):
            k = base + i
            cut = slice(i * width, (i + 1) * width)
            for part, out in ((up_part, outs[: len(outs) // 2]), (down_part, outs[len(outs) // 2 :])):
                block = part[:, cut].astype(jnp.bfloat16)
                if split:
                    half = width // 2
                    first = me[0] == 0
                    out[0][0, k] = jnp.where(first, block[:half], block[half:])
                    out[1][0, k] = jnp.where(first, block[half:], block[:half])
                else:
                    out[0][0, k] = block
            shard, at = place(up_cols[row, k])
            acc[shard, :, at] += back[:, cut]

    @pl.when(row == pl.num_programs(0) - 1)
    def _():
        for s in range(acc.shape[0]):
            in_ref[s] = acc[s].astype(jnp.bfloat16)


def rows_call(split, whole_x, whole_dy, up_blocks, up_cols, down_blocks, down_cols):
    rows, count, width, _ = up_blocks.shape
    shards, tok, part = whole_x.shape
    out_h = width // 2 if split else width
    n_out = 4 if split else 2
    whole = pl.BlockSpec(memory_space=pltpu.VMEM)
    smem = pl.BlockSpec(memory_space=pltpu.SMEM)

    def block(h):
        return pl.BlockSpec((1, count, h, width), lambda r: (r, 0, 0, 0))

    me = lax.axis_index("dp").astype(jnp.int32).reshape(1)
    flops = 10 * tok * rows * count * width * width
    return pl.pallas_call(
        functools.partial(rows_kernel, split),
        grid=(rows,),
        in_specs=[smem, smem, smem, whole, whole, block(width), block(width)],
        out_specs=[whole] + [block(out_h)] * n_out,
        out_shape=[jax.ShapeDtypeStruct(whole_x.shape, jnp.bfloat16)]
        + [jax.ShapeDtypeStruct((rows, count, out_h, width), jnp.bfloat16)] * n_out,
        scratch_shapes=[
            pltpu.VMEM(whole_x.shape, jnp.float32),
            pltpu.VMEM((tok, count * width), jnp.bfloat16),
            pltpu.VMEM((tok, count * width), jnp.bfloat16),
            pltpu.VMEM((width, count * width), jnp.bfloat16),
            pltpu.VMEM((width, count * width), jnp.bfloat16),
        ],
        compiler_params=pltpu.CompilerParams(
            dimension_semantics=("arbitrary",), vmem_limit_bytes=56 * 2**20
        ),
        cost_estimate=pl.CostEstimate(
            flops=flops, bytes_accessed=30 * 2**20, transcendentals=rows * width * tok
        ),
    )(up_cols, down_cols, me, whole_x, whole_dy, up_blocks, down_blocks)


MESH = pl.DeviceIdType.MESH
ALONG_UP, ALONG_DOWN, ACROSS, SIDE = range(4)


def gather_kernel(n_chip, x_ref, dy_ref, x_out, dy_out, send_sem, recv_sem, own_sem):
    hst, z = lax.axis_index("hst"), lax.axis_index("chip")
    far, c = hst // 2, hst % 2
    own = hst * n_chip + z
    ins, outs = (x_ref, dy_ref), (x_out, dy_out)
    not_last, not_first = z < n_chip - 1, z > 0
    peers = {
        ALONG_UP: {"hst": hst, "chip": (z + 1) % n_chip},
        ALONG_DOWN: {"hst": hst, "chip": (z + n_chip - 1) % n_chip},
        ACROSS: {"hst": (1 - far) * 2 + c, "chip": z},
        SIDE: {"hst": far * 2 + 1 - c, "chip": z},
    }

    barrier = pltpu.get_barrier_semaphore()

    def greet(way):
        pl.semaphore_signal(barrier, inc=1, device_id=peers[way], device_id_type=MESH)

    greet(ACROSS)
    greet(SIDE)
    pl.when(not_last)(lambda: greet(ALONG_UP))
    pl.when(not_first)(lambda: greet(ALONG_DOWN))
    inner = jnp.logical_and(not_last, not_first)
    pl.when(inner)(lambda: pl.semaphore_wait(barrier, 4))
    pl.when(jnp.logical_not(inner))(lambda: pl.semaphore_wait(barrier, 3))

    def copy(a, way, shard, source=None):
        return pltpu.make_async_remote_copy(
            src_ref=outs[a].at[shard] if source is None else source,
            dst_ref=outs[a].at[shard],
            send_sem=send_sem.at[a, way, shard],
            recv_sem=recv_sem.at[a, shard],
            device_id=peers[way],
            device_id_type=MESH,
        )

    def each(act):
        for t in range(n_chip + 1):
            for a in range(2):
                if t == 0:
                    act(a, (), own, None, True)
                elif t < n_chip:
                    below = z - t
                    act(a, (ALONG_UP,), hst * n_chip + below, below >= 0, False)
                    above = z + t
                    act(a, (ALONG_DOWN,), hst * n_chip + above, above < n_chip, False)
            for a in range(2):
                if t >= 1:
                    base = ((1 - far) * 2 + c) * n_chip
                    if t == 1:
                        act(a, None, base + z, None, False)
                    else:
                        act(a, None, base + z - (t - 1), z - (t - 1) >= 0, False)
                        act(a, None, base + z + (t - 1), z + (t - 1) < n_chip, False)

    def guarded(condition, run):
        if condition is None:
            run()
        else:
            pl.when(condition)(run)

    def forward(a, ways, shard, condition, is_own):
        def run():
            if not is_own:
                copy(a, SIDE, shard).wait_recv()
            source = ins[a] if is_own else None
            if ways is not None:
                if is_own or ALONG_UP in ways:
                    pl.when(not_last)(lambda: copy(a, ALONG_UP, shard, source).start())
                if is_own or ALONG_DOWN in ways:
                    pl.when(not_first)(lambda: copy(a, ALONG_DOWN, shard, source).start())
                copy(a, ACROSS, shard, source).start()
            copy(a, SIDE, shard, source).start()

        guarded(condition, run)

    def finish(a, ways, shard, condition, is_own):
        def run():
            source = ins[a] if is_own else None
            if ways is not None:
                if is_own or ALONG_UP in ways:
                    pl.when(not_last)(lambda: copy(a, ALONG_UP, shard, source).wait_send())
                if is_own or ALONG_DOWN in ways:
                    pl.when(not_first)(lambda: copy(a, ALONG_DOWN, shard, source).wait_send())
                copy(a, ACROSS, shard, source).wait_send()
            copy(a, SIDE, shard, source).wait_send()

        guarded(condition, run)

    each(forward)
    mine = [pltpu.make_async_copy(ins[a], outs[a].at[own], own_sem.at[a]) for a in range(2)]
    for m in mine:
        m.start()
    for half in range(2):
        for place in range(n_chip):
            for a in range(2):
                copy(a, SIDE, (half * 2 + 1 - c) * n_chip + place).wait_recv()
    each(finish)
    for m in mine:
        m.wait()


def gather_call(n_hst, n_chip, tokens, out_grad):
    if n_hst != 4:
        return [
            lax.all_gather(v, ("hst", "chip"), axis=0, tiled=False) for v in (tokens, out_grad)
        ]
    shards = n_hst * n_chip
    return pl.pallas_call(
        functools.partial(gather_kernel, n_chip),
        in_specs=[pl.BlockSpec(memory_space=pltpu.VMEM)] * 2,
        out_specs=[pl.BlockSpec(memory_space=pl.ANY)] * 2,
        out_shape=[jax.ShapeDtypeStruct((shards, *v.shape), v.dtype) for v in (tokens, out_grad)],
        scratch_shapes=[
            pltpu.SemaphoreType.DMA((2, 4, shards)),
            pltpu.SemaphoreType.DMA((2, shards)),
            pltpu.SemaphoreType.DMA((2,)),
        ],
        compiler_params=pltpu.CompilerParams(collective_id=0, has_side_effects=True),
    )(tokens, out_grad)


def local(n_dp, n_hst, n_chip, tokens, out_grad, up_blocks, up_cols, down_blocks, down_cols):
    whole_x, whole_dy = gather_call(n_hst, n_chip, tokens, out_grad)
    split = n_dp == 2
    partial_value, *grads = rows_call(
        split, whole_x, whole_dy, up_blocks, up_cols, down_blocks, down_cols
    )
    if split:
        swap = [(0, 1), (1, 0)]
        sums = [
            grads[i].astype(jnp.float32)
            + lax.ppermute(grads[i + 1], "dp", swap).astype(jnp.float32)
            for i in (0, 2)
        ]
    else:
        sums = [
            lax.psum_scatter(g, "dp", scatter_dimension=2, tiled=True).astype(jnp.float32)
            for g in grads
        ]
    summed = lax.psum_scatter(
        partial_value, ("hst", "chip"), scatter_dimension=0, tiled=False
    )
    return (summed, *sums)


def solution(mesh):
    placed = (
        P("dp", ("hst", "chip")),
        P("dp", ("hst", "chip")),
        P(("hst", "chip"), None, None, None),
        P(("hst", "chip"), None),
        P(("hst", "chip"), None, None, None),
        P(("hst", "chip"), None),
    )
    return jax.shard_map(
        functools.partial(local, mesh.shape["dp"], mesh.shape["hst"], mesh.shape["chip"]),
        mesh=mesh,
        in_specs=placed,
        out_specs=(
            P("dp", ("hst", "chip")),
            P(("hst", "chip"), None, "dp", None),
            P(("hst", "chip"), None, "dp", None),
        ),
        check_vma=False,
    )
```

```python
import functools

import jax
import jax.numpy as jnp
from jax import lax
from jax.experimental import pallas as pl
from jax.experimental.pallas import tpu as pltpu
from jax.sharding import PartitionSpec as P

NT = (((1,), (1,)), ((), ()))


def rows_kernel(
    split,
    up_cols,
    down_cols,
    me,
    x_ref,
    dy_ref,
    up_ref,
    down_ref,
    in_ref,
    *rest,
):
    outs, (acc, xs, dys, us, ds) = rest[:-5], rest[-5:]
    row = pl.program_id(0)
    width = up_ref.shape[-1]
    per_shard = x_ref.shape[2] // width
    count = up_ref.shape[1]

    @pl.when(row == 0)
    def _():
        acc[...] = jnp.zeros_like(acc)

    def place(col):
        return col // per_shard, pl.ds(pl.multiple_of((col % per_shard) * width, width), width)

    for k in range(count):
        lanes = pl.ds(k * width, width)
        shard, at = place(up_cols[row, k])
        xs[:, lanes] = x_ref[shard, :, at]
        shard, at = place(down_cols[row, k])
        dys[:, lanes] = dy_ref[shard, :, at]
        us[:, lanes] = up_ref[0, k]
        ds[:, lanes] = down_ref[0, k]
    pre = lax.dot_general(us[...], xs[...], NT, preferred_element_type=jnp.float32)
    hid = lax.dot_general(ds[...], dys[...], NT, preferred_element_type=jnp.float32)
    sig = 1.0 / (1.0 + jnp.exp(-pre))
    act = (pre * sig).astype(jnp.bfloat16)
    pre_grad_f = hid * sig * (1.0 + pre * (1.0 - sig))
    pre_grad = pre_grad_f.astype(jnp.bfloat16)
    pre_grad_t = pre_grad_f.T.astype(jnp.bfloat16)

    step = 4
    for base in range(0, count, step):
        lanes = pl.ds(base * width, step * width)
        up_part = jnp.dot(pre_grad, xs[:, lanes], preferred_element_type=jnp.float32)
        down_part = jnp.dot(act, dys[:, lanes], preferred_element_type=jnp.float32)
        back = jnp.dot(pre_grad_t, us[:, lanes], preferred_element_type=jnp.float32)
        for i in range(step):
            k = base + i
            cut = slice(i * width, (i + 1) * width)
            for part, out in ((up_part, outs[: len(outs) // 2]), (down_part, outs[len(outs) // 2 :])):
                block = part[:, cut].astype(jnp.bfloat16)
                if split:
                    half = width // 2
                    first = me[0] == 0
                    out[0][0, k] = jnp.where(first, block[:half], block[half:])
                    out[1][0, k] = jnp.where(first, block[half:], block[:half])
                else:
                    out[0][0, k] = block
            shard, at = place(up_cols[row, k])
            acc[shard, :, at] += back[:, cut]

    @pl.when(row == pl.num_programs(0) - 1)
    def _():
        for s in range(acc.shape[0]):
            in_ref[s] = acc[s].astype(jnp.bfloat16)


def rows_call(split, whole_x, whole_dy, up_blocks, up_cols, down_blocks, down_cols):
    rows, count, width, _ = up_blocks.shape
    shards, tok, part = whole_x.shape
    out_h = width // 2 if split else width
    n_out = 4 if split else 2
    whole = pl.BlockSpec(memory_space=pltpu.VMEM)
    smem = pl.BlockSpec(memory_space=pltpu.SMEM)

    def block(h):
        return pl.BlockSpec((1, count, h, width), lambda r: (r, 0, 0, 0))

    me = lax.axis_index("dp").astype(jnp.int32).reshape(1)
    flops = 10 * tok * rows * count * width * width
    return pl.pallas_call(
        functools.partial(rows_kernel, split),
        grid=(rows,),
        in_specs=[smem, smem, smem, whole, whole, block(width), block(width)],
        out_specs=[whole] + [block(out_h)] * n_out,
        out_shape=[jax.ShapeDtypeStruct(whole_x.shape, jnp.bfloat16)]
        + [jax.ShapeDtypeStruct((rows, count, out_h, width), jnp.bfloat16)] * n_out,
        scratch_shapes=[
            pltpu.VMEM(whole_x.shape, jnp.float32),
            pltpu.VMEM((tok, count * width), jnp.bfloat16),
            pltpu.VMEM((tok, count * width), jnp.bfloat16),
            pltpu.VMEM((width, count * width), jnp.bfloat16),
            pltpu.VMEM((width, count * width), jnp.bfloat16),
        ],
        compiler_params=pltpu.CompilerParams(
            dimension_semantics=("arbitrary",), vmem_limit_bytes=56 * 2**20
        ),
        cost_estimate=pl.CostEstimate(
            flops=flops, bytes_accessed=30 * 2**20, transcendentals=rows * width * tok
        ),
    )(up_cols, down_cols, me, whole_x, whole_dy, up_blocks, down_blocks)


MESH = pl.DeviceIdType.MESH
ALONG_UP, ALONG_DOWN, ACROSS, SIDE = range(4)


def gather_kernel(n_chip, x_ref, dy_ref, x_out, dy_out, send_sem, recv_sem, own_sem):
    hst, z = lax.axis_index("hst"), lax.axis_index("chip")
    far, c = hst // 2, hst % 2
    own = hst * n_chip + z
    ins, outs = (x_ref, dy_ref), (x_out, dy_out)
    not_last, not_first = z < n_chip - 1, z > 0
    peers = {
        ALONG_UP: {"hst": hst, "chip": (z + 1) % n_chip},
        ALONG_DOWN: {"hst": hst, "chip": (z + n_chip - 1) % n_chip},
        ACROSS: {"hst": (1 - far) * 2 + c, "chip": z},
        SIDE: {"hst": far * 2 + 1 - c, "chip": z},
    }

    barrier = pltpu.get_barrier_semaphore()

    def greet(way):
        pl.semaphore_signal(barrier, inc=1, device_id=peers[way], device_id_type=MESH)

    greet(ACROSS)
    greet(SIDE)
    pl.when(not_last)(lambda: greet(ALONG_UP))
    pl.when(not_first)(lambda: greet(ALONG_DOWN))
    inner = jnp.logical_and(not_last, not_first)
    pl.when(inner)(lambda: pl.semaphore_wait(barrier, 4))
    pl.when(jnp.logical_not(inner))(lambda: pl.semaphore_wait(barrier, 3))

    def copy(a, way, shard, source=None):
        return pltpu.make_async_remote_copy(
            src_ref=outs[a].at[shard] if source is None else source,
            dst_ref=outs[a].at[shard],
            send_sem=send_sem.at[a, way, shard],
            recv_sem=recv_sem.at[a, shard],
            device_id=peers[way],
            device_id_type=MESH,
        )

    def each(act):
        for t in range(n_chip + 1):
            for a in range(2):
                if t == 0:
                    act(a, (), own, None, True)
                elif t < n_chip:
                    below = z - t
                    act(a, (ALONG_UP,), hst * n_chip + below, below >= 0, False)
                    above = z + t
                    act(a, (ALONG_DOWN,), hst * n_chip + above, above < n_chip, False)
            for a in range(2):
                if t >= 1:
                    base = ((1 - far) * 2 + c) * n_chip
                    if t == 1:
                        act(a, None, base + z, None, False)
                    else:
                        act(a, None, base + z - (t - 1), z - (t - 1) >= 0, False)
                        act(a, None, base + z + (t - 1), z + (t - 1) < n_chip, False)

    def guarded(condition, run):
        if condition is None:
            run()
        else:
            pl.when(condition)(run)

    def forward(a, ways, shard, condition, is_own):
        def run():
            if not is_own:
                copy(a, SIDE, shard).wait_recv()
            source = ins[a] if is_own else None
            if ways is not None:
                if is_own or ALONG_UP in ways:
                    pl.when(not_last)(lambda: copy(a, ALONG_UP, shard, source).start())
                if is_own or ALONG_DOWN in ways:
                    pl.when(not_first)(lambda: copy(a, ALONG_DOWN, shard, source).start())
                copy(a, ACROSS, shard, source).start()
            copy(a, SIDE, shard, source).start()

        guarded(condition, run)

    def finish(a, ways, shard, condition, is_own):
        def run():
            source = ins[a] if is_own else None
            if ways is not None:
                if is_own or ALONG_UP in ways:
                    pl.when(not_last)(lambda: copy(a, ALONG_UP, shard, source).wait_send())
                if is_own or ALONG_DOWN in ways:
                    pl.when(not_first)(lambda: copy(a, ALONG_DOWN, shard, source).wait_send())
                copy(a, ACROSS, shard, source).wait_send()
            copy(a, SIDE, shard, source).wait_send()

        guarded(condition, run)

    each(forward)
    mine = [pltpu.make_async_copy(ins[a], outs[a].at[own], own_sem.at[a]) for a in range(2)]
    for m in mine:
        m.start()
    for half in range(2):
        for place in range(n_chip):
            for a in range(2):
                copy(a, SIDE, (half * 2 + 1 - c) * n_chip + place).wait_recv()
    each(finish)
    for m in mine:
        m.wait()


def gather_call(n_hst, n_chip, tokens, out_grad):
    if n_hst != 4:
        return [
            lax.all_gather(v, ("hst", "chip"), axis=0, tiled=False) for v in (tokens, out_grad)
        ]
    shards = n_hst * n_chip
    return pl.pallas_call(
        functools.partial(gather_kernel, n_chip),
        in_specs=[pl.BlockSpec(memory_space=pltpu.VMEM)] * 2,
        out_specs=[pl.BlockSpec(memory_space=pl.ANY)] * 2,
        out_shape=[jax.ShapeDtypeStruct((shards, *v.shape), v.dtype) for v in (tokens, out_grad)],
        scratch_shapes=[
            pltpu.SemaphoreType.DMA((2, 4, shards)),
            pltpu.SemaphoreType.DMA((2, shards)),
            pltpu.SemaphoreType.DMA((2,)),
        ],
        compiler_params=pltpu.CompilerParams(collective_id=0, has_side_effects=True),
    )(tokens, out_grad)


def scatter_kernel(n_chip, part, out, side, cross, up, down, cross_out, line_out, send_sem, recv_sem):
    hst, z = lax.axis_index("hst"), lax.axis_index("chip")
    far, c = hst // 2, hst % 2
    not_last, not_first = z < n_chip - 1, z > 0
    peers = {
        ALONG_UP: {"hst": hst, "chip": (z + 1) % n_chip},
        ALONG_DOWN: {"hst": hst, "chip": (z + n_chip - 1) % n_chip},
        ACROSS: {"hst": (1 - far) * 2 + c, "chip": z},
        SIDE: {"hst": far * 2 + 1 - c, "chip": z},
    }
    barrier = pltpu.get_barrier_semaphore()

    def greet(way):
        pl.semaphore_signal(barrier, inc=1, device_id=peers[way], device_id_type=MESH)

    greet(ACROSS)
    greet(SIDE)
    pl.when(not_last)(lambda: greet(ALONG_UP))
    pl.when(not_first)(lambda: greet(ALONG_DOWN))
    inner = jnp.logical_and(not_last, not_first)
    pl.when(inner)(lambda: pl.semaphore_wait(barrier, 4))
    pl.when(jnp.logical_not(inner))(lambda: pl.semaphore_wait(barrier, 3))

    def copy(way, source, target, slot):
        return pltpu.make_async_remote_copy(
            src_ref=source,
            dst_ref=target,
            send_sem=send_sem.at[way, slot],
            recv_sem=recv_sem.at[way, slot],
            device_id=peers[way],
            device_id_type=MESH,
        )

    def side_copy(half, place):
        slot = half * n_chip + place
        return copy(SIDE, part.at[(half * 2 + 1 - c) * n_chip + place], side.at[slot], slot)

    def cross_copy(place):
        return copy(ACROSS, cross_out.at[place], cross.at[place], place)

    def up_copy(place):
        return copy(ALONG_UP, line_out.at[place], up.at[place], place)

    def down_copy(place):
        return copy(ALONG_DOWN, line_out.at[place], down.at[place], place)

    def each(act):
        for t in range(n_chip - 1, 0, -1):
            pl.when(z + t < n_chip)(lambda t=t: act(z + t, 1))
            pl.when(z - t >= 0)(lambda t=t: act(z - t, -1))
        act(z, 0)

    rows = part.shape[1]
    chunk = 32 if rows % 32 == 0 else rows

    def total(store, terms):
        def body(i, carry):
            at = pl.ds(pl.multiple_of(i * chunk, chunk), chunk)
            value = None
            for ref, slot in terms:
                term = ref[slot, at, :].astype(jnp.float32)
                value = term if value is None else value + term
            store(at, value.astype(jnp.bfloat16))
            return carry

        lax.fori_loop(0, rows // chunk, body, 0)

    def to(ref, slot):
        def store(at, value):
            ref[slot, at, :] = value

        return store

    def to_out(at, value):
        out[at, :] = value

    each(lambda place, _: side_copy(1 - far, place).start())
    each(lambda place, _: side_copy(far, place).start())

    def cross_step(place, _):
        slot = (1 - far) * n_chip + place
        side_copy(1 - far, place).wait_recv()
        total(to(cross_out, place), [(part, ((1 - far) * 2 + c) * n_chip + place), (side, slot)])
        cross_copy(place).start()

    each(cross_step)

    def line_step(place, sign):
        slot = far * n_chip + place
        side_copy(far, place).wait_recv()
        cross_copy(place).wait_recv()
        base = [(part, (far * 2 + c) * n_chip + place), (side, slot), (cross, place)]
        if sign > 0:

            @pl.when(not_first)
            def _():
                up_copy(place).wait_recv()
                total(to(line_out, place), base + [(up, place)])

            @pl.when(jnp.logical_not(not_first))
            def _():
                total(to(line_out, place), base)

            up_copy(place).start()
        elif sign < 0:

            @pl.when(not_last)
            def _():
                down_copy(place).wait_recv()
                total(to(line_out, place), base + [(down, place)])

            @pl.when(jnp.logical_not(not_last))
            def _():
                total(to(line_out, place), base)

            down_copy(place).start()
        else:

            @pl.when(inner)
            def _():
                up_copy(place).wait_recv()
                down_copy(place).wait_recv()
                total(to_out, base + [(up, place), (down, place)])

            @pl.when(jnp.logical_not(not_first))
            def _():
                down_copy(place).wait_recv()
                total(to_out, base + [(down, place)])

            @pl.when(jnp.logical_not(not_last))
            def _():
                up_copy(place).wait_recv()
                total(to_out, base + [(up, place)])

    each(line_step)

    def finish(place, sign):
        side_copy(1 - far, place).wait_send()
        side_copy(far, place).wait_send()
        cross_copy(place).wait_send()
        if sign > 0:
            up_copy(place).wait_send()
        elif sign < 0:
            down_copy(place).wait_send()

    each(finish)


def scatter_call(n_hst, n_chip, part):
    if n_hst != 4 or n_chip < 2:
        return lax.psum_scatter(part, ("hst", "chip"), scatter_dimension=0, tiled=False)
    shards, rows, width = part.shape
    whole = pl.BlockSpec(memory_space=pltpu.VMEM)

    def slots(count):
        return pltpu.VMEM((count, rows, width), jnp.bfloat16)

    return pl.pallas_call(
        functools.partial(scatter_kernel, n_chip),
        in_specs=[whole],
        out_specs=whole,
        out_shape=jax.ShapeDtypeStruct((rows, width), jnp.bfloat16),
        scratch_shapes=[slots(2 * n_chip)]
        + [slots(n_chip)] * 5
        + [pltpu.SemaphoreType.DMA((4, 2 * n_chip))] * 2,
        compiler_params=pltpu.CompilerParams(
            collective_id=1, has_side_effects=True, vmem_limit_bytes=24 * 2**20
        ),
        cost_estimate=pl.CostEstimate(
            flops=shards * rows * width, bytes_accessed=120 * 2**20, transcendentals=0
        ),
    )(part)


def local(n_dp, n_hst, n_chip, tokens, out_grad, up_blocks, up_cols, down_blocks, down_cols):
    whole_x, whole_dy = gather_call(n_hst, n_chip, tokens, out_grad)
    split = n_dp == 2
    partial_value, *grads = rows_call(
        split, whole_x, whole_dy, up_blocks, up_cols, down_blocks, down_cols
    )
    if split:
        swap = [(0, 1), (1, 0)]
        sums = [
            grads[i].astype(jnp.float32)
            + lax.ppermute(grads[i + 1], "dp", swap).astype(jnp.float32)
            for i in (0, 2)
        ]
    else:
        sums = [
            lax.psum_scatter(g, "dp", scatter_dimension=2, tiled=True).astype(jnp.float32)
            for g in grads
        ]
    summed = scatter_call(n_hst, n_chip, partial_value)
    return (summed, *sums)


def solution(mesh):
    placed = (
        P("dp", ("hst", "chip")),
        P("dp", ("hst", "chip")),
        P(("hst", "chip"), None, None, None),
        P(("hst", "chip"), None),
        P(("hst", "chip"), None, None, None),
        P(("hst", "chip"), None),
    )
    return jax.shard_map(
        functools.partial(local, mesh.shape["dp"], mesh.shape["hst"], mesh.shape["chip"]),
        mesh=mesh,
        in_specs=placed,
        out_specs=(
            P("dp", ("hst", "chip")),
            P(("hst", "chip"), None, "dp", None),
            P(("hst", "chip"), None, "dp", None),
        ),
        check_vma=False,
    )
```

```python
import functools

import jax
import jax.numpy as jnp
from jax import lax
from jax.experimental import pallas as pl
from jax.experimental.pallas import tpu as pltpu
from jax.sharding import PartitionSpec as P

NT = (((1,), (1,)), ((), ()))


def rows_kernel(
    split,
    up_cols,
    down_cols,
    me,
    x_ref,
    dy_ref,
    up_ref,
    down_ref,
    in_ref,
    *rest,
):
    outs, (acc, xs, dys, us, ds) = rest[:-5], rest[-5:]
    row = pl.program_id(0)
    width = up_ref.shape[-1]
    per_shard = x_ref.shape[2] // width
    count = up_ref.shape[1]

    @pl.when(row == 0)
    def _():
        acc[...] = jnp.zeros_like(acc)

    def place(col):
        return col // per_shard, pl.ds(pl.multiple_of((col % per_shard) * width, width), width)

    for k in range(count):
        lanes = pl.ds(k * width, width)
        shard, at = place(up_cols[row, k])
        xs[:, lanes] = x_ref[shard, :, at]
        shard, at = place(down_cols[row, k])
        dys[:, lanes] = dy_ref[shard, :, at]
        us[:, lanes] = up_ref[0, k]
        ds[:, lanes] = down_ref[0, k]
    pre = lax.dot_general(us[...], xs[...], NT, preferred_element_type=jnp.float32)
    hid = lax.dot_general(ds[...], dys[...], NT, preferred_element_type=jnp.float32)
    sig = 1.0 / (1.0 + jnp.exp(-pre))
    act = (pre * sig).astype(jnp.bfloat16)
    pre_grad_f = hid * sig * (1.0 + pre * (1.0 - sig))
    pre_grad = pre_grad_f.astype(jnp.bfloat16)
    pre_grad_t = pre_grad_f.T.astype(jnp.bfloat16)

    step = 4
    for base in range(0, count, step):
        lanes = pl.ds(base * width, step * width)
        up_part = jnp.dot(pre_grad, xs[:, lanes], preferred_element_type=jnp.float32)
        down_part = jnp.dot(act, dys[:, lanes], preferred_element_type=jnp.float32)
        back = jnp.dot(pre_grad_t, us[:, lanes], preferred_element_type=jnp.float32)
        for i in range(step):
            k = base + i
            cut = slice(i * width, (i + 1) * width)
            for part, out in ((up_part, outs[: len(outs) // 2]), (down_part, outs[len(outs) // 2 :])):
                block = part[:, cut].astype(jnp.bfloat16)
                if split:
                    half = width // 2
                    first = me[0] == 0
                    out[0][0, k] = jnp.where(first, block[:half], block[half:])
                    out[1][0, k] = jnp.where(first, block[half:], block[:half])
                else:
                    out[0][0, k] = block
            shard, at = place(up_cols[row, k])
            acc[shard, :, at] += back[:, cut]

    @pl.when(row == pl.num_programs(0) - 1)
    def _():
        for s in range(acc.shape[0]):
            in_ref[s] = acc[s].astype(jnp.bfloat16)


def rows_call(split, whole_x, whole_dy, up_blocks, up_cols, down_blocks, down_cols):
    rows, count, width, _ = up_blocks.shape
    shards, tok, part = whole_x.shape
    out_h = width // 2 if split else width
    n_out = 4 if split else 2
    whole = pl.BlockSpec(memory_space=pltpu.VMEM)
    smem = pl.BlockSpec(memory_space=pltpu.SMEM)

    def block(h):
        return pl.BlockSpec((1, count, h, width), lambda r: (r, 0, 0, 0))

    me = lax.axis_index("dp").astype(jnp.int32).reshape(1)
    flops = 10 * tok * rows * count * width * width
    return pl.pallas_call(
        functools.partial(rows_kernel, split),
        grid=(rows,),
        in_specs=[smem, smem, smem, whole, whole, block(width), block(width)],
        out_specs=[whole] + [block(out_h)] * n_out,
        out_shape=[jax.ShapeDtypeStruct(whole_x.shape, jnp.bfloat16)]
        + [jax.ShapeDtypeStruct((rows, count, out_h, width), jnp.bfloat16)] * n_out,
        scratch_shapes=[
            pltpu.VMEM(whole_x.shape, jnp.float32),
            pltpu.VMEM((tok, count * width), jnp.bfloat16),
            pltpu.VMEM((tok, count * width), jnp.bfloat16),
            pltpu.VMEM((width, count * width), jnp.bfloat16),
            pltpu.VMEM((width, count * width), jnp.bfloat16),
        ],
        compiler_params=pltpu.CompilerParams(
            dimension_semantics=("arbitrary",), vmem_limit_bytes=56 * 2**20
        ),
        cost_estimate=pl.CostEstimate(
            flops=flops, bytes_accessed=30 * 2**20, transcendentals=rows * width * tok
        ),
    )(up_cols, down_cols, me, whole_x, whole_dy, up_blocks, down_blocks)


MESH = pl.DeviceIdType.MESH
ALONG_UP, ALONG_DOWN, ACROSS, SIDE = range(4)


def gather_kernel(n_chip, x_ref, dy_ref, x_out, dy_out, send_sem, recv_sem, own_sem):
    hst, z = lax.axis_index("hst"), lax.axis_index("chip")
    far, c = hst // 2, hst % 2
    own = hst * n_chip + z
    ins, outs = (x_ref, dy_ref), (x_out, dy_out)
    not_last, not_first = z < n_chip - 1, z > 0
    peers = {
        ALONG_UP: {"hst": hst, "chip": (z + 1) % n_chip},
        ALONG_DOWN: {"hst": hst, "chip": (z + n_chip - 1) % n_chip},
        ACROSS: {"hst": (1 - far) * 2 + c, "chip": z},
        SIDE: {"hst": far * 2 + 1 - c, "chip": z},
    }

    barrier = pltpu.get_barrier_semaphore()

    def greet(way):
        pl.semaphore_signal(barrier, inc=1, device_id=peers[way], device_id_type=MESH)

    greet(ACROSS)
    greet(SIDE)
    pl.when(not_last)(lambda: greet(ALONG_UP))
    pl.when(not_first)(lambda: greet(ALONG_DOWN))
    inner = jnp.logical_and(not_last, not_first)
    pl.when(inner)(lambda: pl.semaphore_wait(barrier, 4))
    pl.when(jnp.logical_not(inner))(lambda: pl.semaphore_wait(barrier, 3))

    def copy(a, way, shard, source=None):
        return pltpu.make_async_remote_copy(
            src_ref=outs[a].at[shard] if source is None else source,
            dst_ref=outs[a].at[shard],
            send_sem=send_sem.at[a, way, shard],
            recv_sem=recv_sem.at[a, shard],
            device_id=peers[way],
            device_id_type=MESH,
        )

    def each(act):
        for t in range(n_chip + 1):
            for a in range(2):
                if t == 0:
                    act(a, (), own, None, True)
                elif t < n_chip:
                    below = z - t
                    act(a, (ALONG_UP,), hst * n_chip + below, below >= 0, False)
                    above = z + t
                    act(a, (ALONG_DOWN,), hst * n_chip + above, above < n_chip, False)
            for a in range(2):
                if t >= 1:
                    base = ((1 - far) * 2 + c) * n_chip
                    if t == 1:
                        act(a, None, base + z, None, False)
                    else:
                        act(a, None, base + z - (t - 1), z - (t - 1) >= 0, False)
                        act(a, None, base + z + (t - 1), z + (t - 1) < n_chip, False)

    def guarded(condition, run):
        if condition is None:
            run()
        else:
            pl.when(condition)(run)

    def forward(a, ways, shard, condition, is_own):
        def run():
            if not is_own:
                copy(a, SIDE, shard).wait_recv()
            source = ins[a] if is_own else None
            if ways is not None:
                if is_own or ALONG_UP in ways:
                    pl.when(not_last)(lambda: copy(a, ALONG_UP, shard, source).start())
                if is_own or ALONG_DOWN in ways:
                    pl.when(not_first)(lambda: copy(a, ALONG_DOWN, shard, source).start())
                copy(a, ACROSS, shard, source).start()
            copy(a, SIDE, shard, source).start()

        guarded(condition, run)

    def finish(a, ways, shard, condition, is_own):
        def run():
            source = ins[a] if is_own else None
            if ways is not None:
                if is_own or ALONG_UP in ways:
                    pl.when(not_last)(lambda: copy(a, ALONG_UP, shard, source).wait_send())
                if is_own or ALONG_DOWN in ways:
                    pl.when(not_first)(lambda: copy(a, ALONG_DOWN, shard, source).wait_send())
                copy(a, ACROSS, shard, source).wait_send()
            copy(a, SIDE, shard, source).wait_send()

        guarded(condition, run)

    each(forward)
    mine = [pltpu.make_async_copy(ins[a], outs[a].at[own], own_sem.at[a]) for a in range(2)]
    for m in mine:
        m.start()
    for half in range(2):
        for place in range(n_chip):
            for a in range(2):
                copy(a, SIDE, (half * 2 + 1 - c) * n_chip + place).wait_recv()
    each(finish)
    for m in mine:
        m.wait()


def gather_call(n_hst, n_chip, tokens, out_grad):
    if n_hst != 4:
        return [
            lax.all_gather(v, ("hst", "chip"), axis=0, tiled=False) for v in (tokens, out_grad)
        ]
    shards = n_hst * n_chip
    return pl.pallas_call(
        functools.partial(gather_kernel, n_chip),
        in_specs=[pl.BlockSpec(memory_space=pltpu.VMEM)] * 2,
        out_specs=[pl.BlockSpec(memory_space=pl.ANY)] * 2,
        out_shape=[jax.ShapeDtypeStruct((shards, *v.shape), v.dtype) for v in (tokens, out_grad)],
        scratch_shapes=[
            pltpu.SemaphoreType.DMA((2, 4, shards)),
            pltpu.SemaphoreType.DMA((2, shards)),
            pltpu.SemaphoreType.DMA((2,)),
        ],
        compiler_params=pltpu.CompilerParams(collective_id=0, has_side_effects=True),
    )(tokens, out_grad)


def scatter_kernel(n_chip, part, out, side, cross, up, down, cross_out, line_out, send_sem, recv_sem):
    hst, z = lax.axis_index("hst"), lax.axis_index("chip")
    far, c = hst // 2, hst % 2
    not_last, not_first = z < n_chip - 1, z > 0
    peers = {
        ALONG_UP: {"hst": hst, "chip": (z + 1) % n_chip},
        ALONG_DOWN: {"hst": hst, "chip": (z + n_chip - 1) % n_chip},
        ACROSS: {"hst": (1 - far) * 2 + c, "chip": z},
        SIDE: {"hst": far * 2 + 1 - c, "chip": z},
    }
    barrier = pltpu.get_barrier_semaphore()

    def greet(way):
        pl.semaphore_signal(barrier, inc=1, device_id=peers[way], device_id_type=MESH)

    greet(ACROSS)
    greet(SIDE)
    pl.when(not_last)(lambda: greet(ALONG_UP))
    pl.when(not_first)(lambda: greet(ALONG_DOWN))
    inner = jnp.logical_and(not_last, not_first)
    pl.when(inner)(lambda: pl.semaphore_wait(barrier, 4))
    pl.when(jnp.logical_not(inner))(lambda: pl.semaphore_wait(barrier, 3))

    def copy(way, source, target, slot):
        return pltpu.make_async_remote_copy(
            src_ref=source,
            dst_ref=target,
            send_sem=send_sem.at[way, slot],
            recv_sem=recv_sem.at[way, slot],
            device_id=peers[way],
            device_id_type=MESH,
        )

    def side_copy(half, place):
        slot = half * n_chip + place
        return copy(SIDE, part.at[(half * 2 + 1 - c) * n_chip + place], side.at[slot], slot)

    def cross_copy(place):
        return copy(ACROSS, cross_out.at[place], cross.at[place], place)

    def up_copy(place):
        return copy(ALONG_UP, line_out.at[place], up.at[place], place)

    def down_copy(place):
        return copy(ALONG_DOWN, line_out.at[place], down.at[place], place)

    def each(act):
        for t in range(n_chip - 1, 0, -1):
            pl.when(z + t < n_chip)(lambda t=t: act(z + t, 1))
            pl.when(z - t >= 0)(lambda t=t: act(z - t, -1))
        act(z, 0)

    rows = part.shape[1]
    chunk = 32 if rows % 32 == 0 else rows

    def total(store, terms):
        def body(i, carry):
            at = pl.ds(pl.multiple_of(i * chunk, chunk), chunk)
            value = None
            for ref, slot in terms:
                term = ref[slot, at, :].astype(jnp.float32)
                value = term if value is None else value + term
            store(at, value.astype(jnp.bfloat16))
            return carry

        lax.fori_loop(0, rows // chunk, body, 0)

    def to(ref, slot):
        def store(at, value):
            ref[slot, at, :] = value

        return store

    def to_out(at, value):
        out[at, :] = value

    each(lambda place, _: side_copy(1 - far, place).start())
    each(lambda place, _: side_copy(far, place).start())

    def cross_step(place, _):
        slot = (1 - far) * n_chip + place
        side_copy(1 - far, place).wait_recv()
        total(to(cross_out, place), [(part, ((1 - far) * 2 + c) * n_chip + place), (side, slot)])
        cross_copy(place).start()

    each(cross_step)

    def line_step(place, sign):
        slot = far * n_chip + place
        side_copy(far, place).wait_recv()
        cross_copy(place).wait_recv()
        base = [(part, (far * 2 + c) * n_chip + place), (side, slot), (cross, place)]
        if sign > 0:

            @pl.when(not_first)
            def _():
                up_copy(place).wait_recv()
                total(to(line_out, place), base + [(up, place)])

            @pl.when(jnp.logical_not(not_first))
            def _():
                total(to(line_out, place), base)

            up_copy(place).start()
        elif sign < 0:

            @pl.when(not_last)
            def _():
                down_copy(place).wait_recv()
                total(to(line_out, place), base + [(down, place)])

            @pl.when(jnp.logical_not(not_last))
            def _():
                total(to(line_out, place), base)

            down_copy(place).start()
        else:

            @pl.when(inner)
            def _():
                up_copy(place).wait_recv()
                down_copy(place).wait_recv()
                total(to_out, base + [(up, place), (down, place)])

            @pl.when(jnp.logical_not(not_first))
            def _():
                down_copy(place).wait_recv()
                total(to_out, base + [(down, place)])

            @pl.when(jnp.logical_not(not_last))
            def _():
                up_copy(place).wait_recv()
                total(to_out, base + [(up, place)])

    each(line_step)

    def finish(place, sign):
        side_copy(1 - far, place).wait_send()
        side_copy(far, place).wait_send()
        cross_copy(place).wait_send()
        if sign > 0:
            up_copy(place).wait_send()
        elif sign < 0:
            down_copy(place).wait_send()

    each(finish)


def scatter_call(n_hst, n_chip, part):
    if n_hst != 4 or n_chip < 2:
        return lax.psum_scatter(part, ("hst", "chip"), scatter_dimension=0, tiled=False)
    shards, rows, width = part.shape
    whole = pl.BlockSpec(memory_space=pltpu.VMEM)

    def slots(count):
        return pltpu.VMEM((count, rows, width), jnp.bfloat16)

    return pl.pallas_call(
        functools.partial(scatter_kernel, n_chip),
        in_specs=[whole],
        out_specs=whole,
        out_shape=jax.ShapeDtypeStruct((rows, width), jnp.bfloat16),
        scratch_shapes=[slots(2 * n_chip)]
        + [slots(n_chip)] * 5
        + [pltpu.SemaphoreType.DMA((4, 2 * n_chip))] * 2,
        compiler_params=pltpu.CompilerParams(
            collective_id=1, has_side_effects=True, vmem_limit_bytes=24 * 2**20
        ),
        cost_estimate=pl.CostEstimate(
            flops=shards * rows * width, bytes_accessed=120 * 2**20, transcendentals=0
        ),
    )(part)


def local(n_dp, n_hst, n_chip, tokens, out_grad, up_blocks, up_cols, down_blocks, down_cols):
    whole_x, whole_dy = gather_call(n_hst, n_chip, tokens, out_grad)
    split = n_dp == 2
    rows = up_blocks.shape[0]
    cuts = [slice(0, rows // 2), slice(rows // 2, rows)] if split else [slice(0, rows)]
    parts, sums = [], [[], []]
    for cut in cuts:
        part, *grads = rows_call(
            split, whole_x, whole_dy, up_blocks[cut], up_cols[cut], down_blocks[cut], down_cols[cut]
        )
        parts.append(part.astype(jnp.float32))
        for i in range(2):
            if split:
                sent = lax.ppermute(grads[2 * i + 1], "dp", [(0, 1), (1, 0)])
                both = grads[2 * i].astype(jnp.float32) + sent.astype(jnp.float32)
            else:
                both = lax.psum_scatter(
                    grads[i], "dp", scatter_dimension=2, tiled=True
                ).astype(jnp.float32)
            sums[i].append(both)
    sums = [jnp.concatenate(pieces, axis=0) for pieces in sums]
    partial_value = sum(parts).astype(jnp.bfloat16)
    summed = scatter_call(n_hst, n_chip, partial_value)
    return (summed, *sums)


def solution(mesh):
    placed = (
        P("dp", ("hst", "chip")),
        P("dp", ("hst", "chip")),
        P(("hst", "chip"), None, None, None),
        P(("hst", "chip"), None),
        P(("hst", "chip"), None, None, None),
        P(("hst", "chip"), None),
    )
    return jax.shard_map(
        functools.partial(local, mesh.shape["dp"], mesh.shape["hst"], mesh.shape["chip"]),
        mesh=mesh,
        in_specs=placed,
        out_specs=(
            P("dp", ("hst", "chip")),
            P(("hst", "chip"), None, "dp", None),
            P(("hst", "chip"), None, "dp", None),
        ),
        check_vma=False,
    )
```
